32 devices in a mesh: row: 8 (over y, x, core), section: 4 (over z).
Axes of the slice: x: 2, y: 2, z: 4, core: 2. Of those that a mesh axis runs over, the one named last changes fastest.
Arguments:
- features: bfloat16 [8192, 256], P('row'), may hold values from -6 to 6
- weight: bfloat16 [256, 256], replicated, may hold values from -0.375 to 0.375
- cotangent: bfloat16 [8192, 256], P('row'), may hold values from -0.0625 to 0.0625
- counts: int32 [64, 16, 128, 128], P('row', 'section'), may hold values from 0 to 3, as said below
- columns: int32 [64, 16], P('row', 'section'), may hold values from 0 to 63, as said below
- live_slots: int32 [64, 4], P('row', 'section'), may hold values from 1 to 4, as said below
Outputs:
- output: bfloat16 [8192, 256], P('row')
- grad_weight: float32 [256, 256], replicated
The draws below stay inside these ranges and needn't reach their ends.
Inputs may be any that keep to these rules, and one draw needn't show every extreme that they name: `columns`: every entry in a slot of section index s names a node block g with (g // 8) % 4 == s; the 4 slots of one row of blocks and one section index name distinct column blocks. Slots at k >= live_slots[b, s] are ignored; the value 4 occurs at every section index in every draw. `counts`: most entries are zero.
All inputs are finite; a program needn't handle non-finite values.
Results may differ from the reference program's by a relative error of at most 0.0055.
Values may be sent and summed in bfloat16 or wider, within the bound.
A program may use at most 64 MiB of HBM per device.

```python
import jax
import jax.numpy as jnp
from jax import lax

F = 256
BLK = 128
RB_DEV = 8
KS = 4
NB = 64
NODES = 8192
SECTIONS = 4


def draw_counts(key, part):
    first_key, second_key = jax.random.split(key, 2)
    shape = (NB, SECTIONS * KS, BLK, BLK)
    present = jax.random.randint(first_key, shape, 0, 3)
    values = jax.random.randint(second_key, shape, 1, 4)
    return jnp.where(present == 0, values, 0).astype(jnp.int32)


def draw_columns(key, part):
    window_blocks = NB // SECTIONS
    row_keys = jax.random.split(key, NB * SECTIONS)

    def pick_distinct(one_key):
        return jax.random.permutation(one_key, window_blocks)[:KS]
    local_block = jax.vmap(pick_distinct)(row_keys).reshape(NB, SECTIONS * KS).astype(jnp.int32)
    section_of_slot = jnp.arange(SECTIONS * KS, dtype=jnp.int32)[None, :] // KS
    owner_turn = local_block // RB_DEV
    inner_block = local_block % RB_DEV
    return ((section_of_slot + SECTIONS * owner_turn) * RB_DEV + inner_block).astype(jnp.int32)


def draw_live_slots(key, part):
    first_key, second_key, third_key, fourth_key = jax.random.split(key, 4)
    heavy_rows = jax.random.randint(first_key, (NB, SECTIONS), KS // 2 + 1, KS + 1)
    light_rows = jax.random.randint(second_key, (NB, SECTIONS), 1, KS // 2 + 1)
    picker = jax.random.randint(third_key, (NB, SECTIONS), 0, 8)
    values = jnp.where(picker == 0, heavy_rows, light_rows)
    chosen_row = jax.random.randint(fourth_key, (SECTIONS,), 0, NB)
    row_ids = jnp.arange(NB, dtype=jnp.int32)[:, None]
    values = jnp.where(row_ids == chosen_row[None, :], KS, values)
    return values.astype(jnp.int32)


def block_scale(key, extent, cuts, least, largest):
    level, own = 1.0, jax.random.fold_in(key, 6)
    for dim, shards_of in cuts:
        steps = jnp.exp(jax.random.uniform(jax.random.fold_in(own, dim), (shards_of,), jnp.float32, least / len(cuts), largest / len(cuts)))
        level = level * jnp.repeat(steps, extent[dim] // shards_of).reshape([-1 if axis == dim else 1 for axis in range(len(extent))])
    return level


def noise(stream_key, shape, spread, most, pieces=(), kind=jnp.bfloat16):
    values = jax.random.normal(stream_key, shape, jnp.float32) * spread
    if len(pieces) > 0:
        values = block_scale(stream_key, shape, pieces, -0.22, 0.18) * values
    return jnp.clip(values, min=-most, max=most).astype(kind)


def setup_inputs(seed: int = 0) -> dict:
    key_list = jax.random.split(jax.random.key(seed), 7)
    features = noise(key_list[0], (NODES, F), 1.0, 6.0, ((0, 8),))
    weight = noise(key_list[1], (F, F), F ** -0.5, 0.375)
    cotangent = noise(key_list[2], (NODES, F), NODES ** -0.5, 0.0625, ((0, 8),))
    counts = draw_counts(jax.random.fold_in(key_list[6], 71), 0)
    columns = draw_columns(jax.random.fold_in(key_list[6], 71), 0)
    live_slots = draw_live_slots(jax.random.fold_in(key_list[6], 71), 0)
    return dict(features=features, weight=weight, cotangent=cotangent, counts=counts, columns=columns, live_slots=live_slots)


def reference(features, weight, cotangent, counts, columns, live_slots):
    feat_width = features.shape[1]
    blocks = features.reshape(NB, BLK, feat_width)
    slot_rank = jnp.arange(SECTIONS * KS, dtype=jnp.int32) % KS
    slot_used = slot_rank[None, :] < jnp.repeat(live_slots, KS, axis=1)

    def one_block(block_items):
        block_counts, block_cols, block_used = block_items
        masked = jnp.where(block_used[:, None, None], block_counts, 0)
        degree = lax.optimization_barrier(jnp.sum(masked, axis=(0, 2))).astype(jnp.float32)
        picked = blocks[block_cols.astype(jnp.int32)].astype(jnp.float32)
        summed = jnp.einsum('kij,kjf->if', masked.astype(jnp.float32), picked)
        return (summed * lax.rsqrt(1.0 + degree)[:, None]).astype(jnp.bfloat16)
    aggregate = lax.map(one_block, (counts, columns, slot_used)).reshape(NODES, feat_width)
    pre_act = jnp.dot(aggregate, weight, preferred_element_type=jnp.float32)
    gate_value = jax.nn.sigmoid(pre_act)
    output = (pre_act * gate_value).astype(jnp.bfloat16)
    grad_pre = (cotangent.astype(jnp.float32) * gate_value * (1.0 + pre_act * (1.0 - gate_value))).astype(jnp.bfloat16)
    grad_weight = lax.dot_general(aggregate, grad_pre, (((0,), (0,)), ((), ())), preferred_element_type=jnp.float32)
    return (output, grad_weight)
```

```python
import functools

import jax
import jax.numpy as jnp
from jax import lax
from jax.experimental import pallas as pl
from jax.experimental.pallas import tpu as pltpu
from jax.sharding import PartitionSpec as P

MESH = pl.DeviceIdType.MESH


def remote(src, dst, send_sem, recv_sem, where):
    return pltpu.make_async_remote_copy(
        src_ref=src, dst_ref=dst, send_sem=send_sem, recv_sem=recv_sem,
        device_id=where, device_id_type=MESH,
    )


def kernel(
    rows, sections, plane,
    live, cols, feat, weight, cot, counts,
    out, gw_out,
    cnt_v, cot_v, w_v, edge, win, deg_all, scale, part32, part16, rs_in,
    gw32, g_send, ga_in, gb_in,
    l_sem, f_ssem, f_rsem, d_ssem, d_rsem, rs_ssem, rs_rsem, o_ssem, o_rsem,
    ga_ssem, ga_rsem, gb_ssem, gb_rsem, gc_ssem, gc_rsem,
):
    row = lax.axis_index("row")
    sec = lax.axis_index("section")
    blocks, slots, size, _ = cnt_v.shape
    width = win.shape[-1]
    turns = rows // sections
    span = rs_in.shape[1]
    grain = gw_out.shape[1]

    loads = [
        pltpu.make_async_copy(counts, cnt_v, l_sem.at[0]),
        pltpu.make_async_copy(weight, w_v, l_sem.at[1]),
        pltpu.make_async_copy(cot.at[sec], cot_v, l_sem.at[2]),
    ]
    for load in loads:
        load.start()

    barrier = pltpu.get_barrier_semaphore()
    for j in range(1, rows):
        pl.semaphore_signal(barrier, inc=1, device_id={"row": lax.rem(row + j, rows)}, device_id_type=MESH)
    for j in range(1, sections):
        pl.semaphore_signal(barrier, inc=1, device_id={"section": lax.rem(sec + j, sections)}, device_id_type=MESH)
    pl.semaphore_wait(barrier, rows - 1 + sections - 1)

    own = [row == t * sections + sec for t in range(turns)]
    keep = [pltpu.make_async_copy(feat, win.at[pl.ds(t * blocks, blocks)], l_sem.at[3]) for t in range(turns)]
    sends = []
    if plane:
        half = blocks // 2
        y, x, c = row // 4, lax.rem(row // 2, 2), lax.rem(row, 2)
        home_x = sec // 2
        sib = row + 1 - 2 * c

        def chunk(t, i, kind, where):
            return remote(
                win.at[t * blocks + i], win.at[t * blocks + i],
                f_ssem.at[kind, t, i], f_rsem.at[t, i], {"row": where},
            )

        for t in range(turns):
            def first(t=t, act="start"):
                for k in range(half):
                    for h in range(2):
                        i = h * half + k
                        for kind, where in (
                            (0, (1 - y) * 4 + x * 2 + h),
                            (1, y * 4 + (1 - x) * 2 + h),
                            (2, sib),
                        ):
                            d = remote(
                                feat.at[i], win.at[t * blocks + i],
                                f_ssem.at[kind, t, i], f_rsem.at[t, i], {"row": where},
                            )
                            if act == "start":
                                d.start()
                            else:
                                d.wait_send()

            @pl.when(own[t])
            def _(first=first, t=t):
                keep[t].start()
                first()

            sends.append((own[t], functools.partial(first, act="wait")))
    else:
        for t in range(turns):
            def direct(j, t):
                return remote(
                    feat, win.at[pl.ds(t * blocks, blocks)],
                    f_ssem.at[t, j], f_rsem.at[t, 0], {"row": lax.rem(row + j, rows)},
                )

            def first(act, t=t, direct=direct):
                def body(j, carry):
                    d = direct(j, t)
                    if act == "start":
                        d.start()
                    else:
                        d.wait_send()
                    return carry
                lax.fori_loop(1, rows, body, 0)

            @pl.when(own[t])
            def _(first=first, t=t):
                keep[t].start()
                first("start")

            sends.append((own[t], functools.partial(first, "wait")))

    loads[0].wait()
    ones = jnp.ones((8, size), jnp.bfloat16)

    def prepare(b, carry):
        total = jnp.zeros((size, size), jnp.int32)
        for k in range(slots):
            e = jnp.where(k < live[b, 0], cnt_v[b, k], 0)
            total = total + e
            edge[b, :, k * size:(k + 1) * size] = e.astype(jnp.float32).astype(jnp.bfloat16)
        d = lax.dot_general(
            ones, total.astype(jnp.float32).astype(jnp.bfloat16), (((1,), (1,)), ((), ())),
            preferred_element_type=jnp.float32,
        )
        deg_all[sec, pl.ds(b, 1), :] = d[0:1]
        return carry

    lax.fori_loop(0, blocks, prepare, 0)
    deg_copies = []
    for j in range(1, sections):
        peer = lax.rem(sec + j, sections)
        d = remote(deg_all.at[sec], deg_all.at[sec], d_ssem.at[j], d_rsem.at[sec], {"section": peer})
        d.start()
        deg_copies.append(d)

    if plane:
        off_chip = [jnp.logical_not((y == t) & (x == home_x)) for t in range(turns)]
        pass_on = [(y == t) & (x != home_x) for t in range(turns)]
        across = (1 - y) * 4 + x * 2 + c
        for k in range(half):
            for t in range(turns):
                i = c * half + k

                @pl.when(off_chip[t])
                def _(i=i, t=t):
                    chunk(t, i, 2, sib).wait_recv()
                    chunk(t, i, 2, sib).start()

                    @pl.when(pass_on[t])
                    def _():
                        chunk(t, i, 0, across).start()
        for t in range(turns):
            def other(t=t):
                for k in range(half):
                    chunk(t, (1 - c) * half + k, 2, sib).wait_recv()

            def mine(t=t):
                for k in range(half):
                    chunk(t, c * half + k, 2, sib).wait_recv()

            @pl.when(jnp.logical_not(own[t]))
            def _(other=other):
                other()

            @pl.when((y == t) & (x == home_x) & jnp.logical_not(own[t]))
            def _(mine=mine):
                mine()

            @pl.when(own[t])
            def _(t=t):
                keep[t].wait()

            def relayed(t=t):
                for k in range(half):
                    chunk(t, c * half + k, 2, sib).wait_send()

            def crossed(t=t):
                for k in range(half):
                    chunk(t, c * half + k, 0, across).wait_send()

            sends.append((off_chip[t], relayed))
            sends.append((pass_on[t], crossed))
    else:
        for t in range(turns):
            @pl.when(own[t])
            def _(t=t):
                keep[t].wait()

            @pl.when(jnp.logical_not(own[t]))
            def _(t=t):
                direct(1, t).wait_recv()

    def block_sum(b):
        acc = jnp.zeros((size, width), jnp.float32)
        for k in range(0, slots, 2):
            picked = []
            for q in (k, k + 1):
                g = cols[b, q]
                picked.append(win[lax.div(lax.div(g, blocks), sections) * blocks + lax.rem(g, blocks)])
            acc = acc + jnp.dot(
                edge[b, :, k * size:(k + 2) * size], jnp.concatenate(picked, axis=0),
                preferred_element_type=jnp.float32,
            )
        at = pl.ds(pl.multiple_of(b * size, size), size)
        part32[at, :] = acc
        part16[at, :] = acc.astype(jnp.bfloat16)

    per = span // size
    if per == 0:
        for b in range(blocks):
            block_sum(b)
    rs_copies = []
    for j in range(1, sections + 1):
        peer = lax.rem(sec + j, sections)
        for q in range(per):
            block_sum(peer * per + q)
        if j < sections:
            d = remote(
                part16.at[pl.ds(pl.multiple_of(peer * span, span), span)], rs_in.at[sec],
                rs_ssem.at[j], rs_rsem.at[sec], {"section": peer},
            )
            d.start()
            rs_copies.append(d)

    for j in range(1, sections):
        peer = lax.rem(sec + j, sections)
        remote(deg_all.at[peer], deg_all.at[peer], d_ssem.at[j], d_rsem.at[peer], {"section": peer}).wait_recv()
    degree = deg_all[0]
    for z in range(1, sections):
        degree = degree + deg_all[z]
    inv = lax.rsqrt(1.0 + degree).T
    for b in range(blocks):
        scale[b * size:(b + 1) * size, :] = jnp.broadcast_to(inv[:, b:b + 1], (size, size))

    mine_at = pl.ds(pl.multiple_of(sec * span, span), span)
    total = part32[mine_at, :]
    for j in range(1, sections):
        peer = lax.rem(sec + j, sections)
        remote(rs_in.at[peer], rs_in.at[peer], rs_ssem.at[j], rs_rsem.at[peer], {"section": peer}).wait_recv()
        total = total + rs_in[peer].astype(jnp.float32)
    own_scale = scale[mine_at, :]
    aggregate = (total * jnp.concatenate([own_scale] * (width // size), axis=1)).astype(jnp.bfloat16)

    loads[1].wait()
    loads[2].wait()
    pre = jnp.dot(aggregate, w_v[...], preferred_element_type=jnp.float32)
    gate = jax.nn.sigmoid(pre)
    out[sec] = (pre * gate).astype(jnp.bfloat16)
    grad_pre = (cot_v[...].astype(jnp.float32) * gate * (1.0 + pre * (1.0 - gate))).astype(jnp.bfloat16)
    grad = lax.dot_general(aggregate, grad_pre, (((0,), (0,)), ((), ())), preferred_element_type=jnp.float32)
    grad = grad.reshape(rows, grain, width)
    gw32[...] = grad
    g_send[...] = grad.astype(jnp.bfloat16)

    tail = []
    for j in range(1, rows):
        peer = lax.rem(row + j, rows)
        d = remote(g_send.at[peer], ga_in.at[row], ga_ssem.at[j], ga_rsem.at[row], {"row": peer})
        d.start()
        tail.append(d)
    out_copies = []
    for j in range(1, sections):
        peer = lax.rem(sec + j, sections)
        d = remote(out.at[sec], out.at[sec], o_ssem.at[j], o_rsem.at[sec], {"section": peer})
        d.start()
        out_copies.append(d)

    acc = gw32[row]
    for j in range(1, rows):
        peer = lax.rem(row + j, rows)
        remote(ga_in.at[peer], ga_in.at[peer], ga_ssem.at[j], ga_rsem.at[peer], {"row": peer}).wait_recv()
        acc = acc + ga_in[peer].astype(jnp.float32)
    gb_in[sec] = acc
    for j in range(1, sections):
        peer = lax.rem(sec + j, sections)
        d = remote(gb_in.at[sec], gb_in.at[sec], gb_ssem.at[j], gb_rsem.at[sec], {"section": peer})
        d.start()
        tail.append(d)
    for j in range(1, sections):
        peer = lax.rem(sec + j, sections)
        remote(gb_in.at[peer], gb_in.at[peer], gb_ssem.at[j], gb_rsem.at[peer], {"section": peer}).wait_recv()
    acc = gb_in[0]
    for z in range(1, sections):
        acc = acc + gb_in[z]
    gw_out[row] = acc
    for j in range(1, rows):
        peer = lax.rem(row + j, rows)
        d = remote(gw_out.at[row], gw_out.at[row], gc_ssem.at[j], gc_rsem.at[row], {"row": peer})
        d.start()
        tail.append(d)
    for j in range(1, rows):
        peer = lax.rem(row + j, rows)
        remote(gw_out.at[peer], gw_out.at[peer], gc_ssem.at[j], gc_rsem.at[peer], {"row": peer}).wait_recv()
    for j in range(1, sections):
        peer = lax.rem(sec + j, sections)
        remote(out.at[peer], out.at[peer], o_ssem.at[j], o_rsem.at[peer], {"section": peer}).wait_recv()

    for cond, finish in sends:
        pl.when(cond)(finish)
    for d in deg_copies + rs_copies + out_copies + tail:
        d.wait_send()


def per_device(rows, sections, plane, features, weight, cotangent, counts, columns, live_slots):
    count, width = features.shape
    blocks, slots, size, _ = counts.shape
    span = count // sections
    grain = width // rows
    turns = rows // sections
    dma = pltpu.SemaphoreType.DMA
    f32, bf16 = jnp.float32, jnp.bfloat16
    any_spec = pl.BlockSpec(memory_space=pl.ANY)
    smem = pl.BlockSpec(memory_space=pltpu.SMEM)
    vmem = pl.BlockSpec(memory_space=pltpu.VMEM)
    out, grad = pl.pallas_call(
        functools.partial(kernel, rows, sections, plane),
        out_shape=(
            jax.ShapeDtypeStruct((sections, span, width), bf16),
            jax.ShapeDtypeStruct((rows, grain, width), f32),
        ),
        in_specs=[smem, smem, any_spec, any_spec, any_spec, any_spec],
        out_specs=(vmem, vmem),
        scratch_shapes=[
            pltpu.VMEM((blocks, slots, size, size), jnp.int32),
            pltpu.VMEM((span, width), bf16),
            pltpu.VMEM((width, width), bf16),
            pltpu.VMEM((blocks, size, slots * size), bf16),
            pltpu.VMEM((turns * blocks, size, width), bf16),
            pltpu.VMEM((sections, blocks, size), f32),
            pltpu.VMEM((count, size), f32),
            pltpu.VMEM((count, width), f32),
            pltpu.VMEM((count, width), bf16),
            pltpu.VMEM((sections, span, width), bf16),
            pltpu.VMEM((rows, grain, width), f32),
            pltpu.VMEM((rows, grain, width), bf16),
            pltpu.VMEM((rows, grain, width), bf16),
            pltpu.VMEM((sections, grain, width), f32),
            dma((4,)),
            dma((3, turns, blocks)) if plane else dma((turns, rows)),
            dma((turns, blocks)),
            dma((sections,)), dma((sections,)),
            dma((sections,)), dma((sections,)),
            dma((sections,)), dma((sections,)),
            dma((rows,)), dma((rows,)),
            dma((sections,)), dma((sections,)),
            dma((rows,)), dma((rows,)),
        ],
        compiler_params=pltpu.CompilerParams(
            collective_id=0, has_side_effects=True, vmem_limit_bytes=40 * 1024 * 1024
        ),
    )(
        live_slots, columns, features.reshape(blocks, size, width), weight,
        cotangent.reshape(sections, span, width), counts,
    )
    return out.reshape(count, width), grad.reshape(width, width)


def solution(mesh):
    rows, sections = mesh.shape["row"], mesh.shape["section"]
    in_specs = (
        P("row", None),
        P(),
        P("row", None),
        P("row", "section", None, None),
        P("row", "section"),
        P("row", "section"),
    )
    out_specs = (P("row", None), P())
    return jax.shard_map(
        functools.partial(per_device, rows, sections, (rows, sections) == (8, 4)),
        mesh=mesh, in_specs=in_specs, out_specs=out_specs, check_vma=False,
    )
```

```python
import functools

import jax
import jax.numpy as jnp
from jax import lax
from jax.experimental import pallas as pl
from jax.experimental.pallas import tpu as pltpu
from jax.sharding import PartitionSpec as P

MESH = pl.DeviceIdType.MESH


def remote(src, dst, send_sem, recv_sem, where):
    return pltpu.make_async_remote_copy(
        src_ref=src, dst_ref=dst, send_sem=send_sem, recv_sem=recv_sem,
        device_id=where, device_id_type=MESH,
    )


def kernel(
    rows, sections, plane,
    live, cols, feat, weight, cot, counts,
    out, gw_out,
    cnt_v, cot_v, w_v, edge, win, deg_all, scale, part32, part16, rs_in,
    gw32, g_send, ga_in, gb_in,
    l_sem, f_ssem, f_rsem, d_ssem, d_rsem, rs_ssem, rs_rsem, o_ssem, o_rsem,
    ga_ssem, ga_rsem, gb_ssem, gb_rsem, gc_ssem, gc_rsem,
):
    row = lax.axis_index("row")
    sec = lax.axis_index("section")
    blocks, slots, size, _ = cnt_v.shape
    width = win.shape[-1]
    turns = rows // sections
    span = rs_in.shape[1]
    grain = gw_out.shape[1]

    loads = [
        pltpu.make_async_copy(counts, cnt_v, l_sem.at[0]),
        pltpu.make_async_copy(weight, w_v, l_sem.at[1]),
        pltpu.make_async_copy(cot.at[sec], cot_v, l_sem.at[2]),
    ]
    for load in loads:
        load.start()

    barrier = pltpu.get_barrier_semaphore()
    for j in range(1, rows):
        pl.semaphore_signal(barrier, inc=1, device_id={"row": lax.rem(row + j, rows)}, device_id_type=MESH)
    for j in range(1, sections):
        pl.semaphore_signal(barrier, inc=1, device_id={"section": lax.rem(sec + j, sections)}, device_id_type=MESH)
    pl.semaphore_wait(barrier, rows - 1 + sections - 1)

    own = [row == t * sections + sec for t in range(turns)]
    keep = [pltpu.make_async_copy(feat, win.at[pl.ds(t * blocks, blocks)], l_sem.at[3]) for t in range(turns)]
    sends = []
    if plane:
        half = blocks // 2
        y, x, c = row // 4, lax.rem(row // 2, 2), lax.rem(row, 2)
        home_x = sec // 2
        sib = row + 1 - 2 * c

        def chunk(t, i, kind, where):
            return remote(
                win.at[t * blocks + i], win.at[t * blocks + i],
                f_ssem.at[kind, t, i], f_rsem.at[t, i], {"row": where},
            )

        for t in range(turns):
            def first(t=t, act="start"):
                for k in range(half):
                    for h in range(2):
                        i = h * half + k
                        for kind, where in (
                            (0, (1 - y) * 4 + x * 2 + h),
                            (1, y * 4 + (1 - x) * 2 + h),
                            (2, sib),
                        ):
                            d = remote(
                                feat.at[i], win.at[t * blocks + i],
                                f_ssem.at[kind, t, i], f_rsem.at[t, i], {"row": where},
                            )
                            if act == "start":
                                d.start()
                            else:
                                d.wait_send()

            @pl.when(own[t])
            def _(first=first, t=t):
                keep[t].start()
                first()

            sends.append((own[t], functools.partial(first, act="wait")))
    else:
        for t in range(turns):
            def direct(j, t):
                return remote(
                    feat, win.at[pl.ds(t * blocks, blocks)],
                    f_ssem.at[t, j], f_rsem.at[t, 0], {"row": lax.rem(row + j, rows)},
                )

            def first(act, t=t, direct=direct):
                def body(j, carry):
                    d = direct(j, t)
                    if act == "start":
                        d.start()
                    else:
                        d.wait_send()
                    return carry
                lax.fori_loop(1, rows, body, 0)

            @pl.when(own[t])
            def _(first=first, t=t):
                keep[t].start()
                first("start")

            sends.append((own[t], functools.partial(first, "wait")))

    loads[0].wait()
    ones = jnp.ones((8, size), jnp.bfloat16)

    def prepare(b, carry):
        total = jnp.zeros((size, size), jnp.int32)
        for k in range(slots):
            e = jnp.where(k < live[0, b], cnt_v[b, k], 0)
            total = total + e
            edge[b, :, k * size:(k + 1) * size] = e.astype(jnp.float32).astype(jnp.bfloat16)
        d = lax.dot_general(
            ones, total.astype(jnp.float32).astype(jnp.bfloat16), (((1,), (1,)), ((), ())),
            preferred_element_type=jnp.float32,
        )
        deg_all[sec, pl.ds(b, 1), :] = d[0:1]
        return carry

    lax.fori_loop(0, blocks, prepare, 0)
    deg_copies = []
    for j in range(1, sections):
        peer = lax.rem(sec + j, sections)
        d = remote(deg_all.at[sec], deg_all.at[sec], d_ssem.at[j], d_rsem.at[sec], {"section": peer})
        d.start()
        deg_copies.append(d)

    if plane:
        across = (1 - y) * 4 + x * 2 + c
        away = x != home_x
        far = 1 - y

        @pl.when(away)
        def _():
            for k in range(half):
                i = c * half + k
                chunk(y, i, 2, sib).wait_recv()
                chunk(y, i, 0, across).start()
                chunk(y, i, 2, sib).start()

        for k in range(half):
            i = c * half + k
            chunk(far, i, 2, sib).wait_recv()
            chunk(far, i, 2, sib).start()
        for k in range(half):
            chunk(far, (1 - c) * half + k, 2, sib).wait_recv()

        @pl.when(away)
        def _():
            for k in range(half):
                chunk(y, (1 - c) * half + k, 2, sib).wait_recv()

        @pl.when((x == home_x) & (c != lax.rem(sec, 2)))
        def _():
            for i in range(blocks):
                chunk(y, i, 2, sib).wait_recv()

        for t in range(turns):
            @pl.when(own[t])
            def _(t=t):
                keep[t].wait()

        def crossed():
            for k in range(half):
                chunk(y, c * half + k, 0, across).wait_send()
                chunk(y, c * half + k, 2, sib).wait_send()

        def relayed():
            for k in range(half):
                chunk(far, c * half + k, 2, sib).wait_send()

        sends.append((away, crossed))
        sends.append((row >= 0, relayed))
    else:
        for t in range(turns):
            @pl.when(own[t])
            def _(t=t):
                keep[t].wait()

            @pl.when(jnp.logical_not(own[t]))
            def _(t=t):
                direct(1, t).wait_recv()

    def block_sum(b):
        acc = jnp.zeros((size, width), jnp.float32)
        for k in range(0, slots, 2):
            picked = []
            for q in (k, k + 1):
                g = cols[q, b]
                picked.append(win[lax.div(lax.div(g, blocks), sections) * blocks + lax.rem(g, blocks)])
            acc = acc + jnp.dot(
                edge[b, :, k * size:(k + 2) * size], jnp.concatenate(picked, axis=0),
                preferred_element_type=jnp.float32,
            )
        at = pl.ds(pl.multiple_of(b * size, size), size)
        part32[at, :] = acc
        part16[at, :] = acc.astype(jnp.bfloat16)

    per = span // size
    if per == 0:
        for b in range(blocks):
            block_sum(b)
    rs_copies = []
    for j in range(1, sections + 1):
        peer = lax.rem(sec + j, sections)
        for q in range(per):
            block_sum(peer * per + q)
        if j < sections:
            d = remote(
                part16.at[pl.ds(pl.multiple_of(peer * span, span), span)], rs_in.at[sec],
                rs_ssem.at[j], rs_rsem.at[sec], {"section": peer},
            )
            d.start()
            rs_copies.append(d)

    for j in range(1, sections):
        peer = lax.rem(sec + j, sections)
        remote(deg_all.at[peer], deg_all.at[peer], d_ssem.at[j], d_rsem.at[peer], {"section": peer}).wait_recv()
    degree = deg_all[0]
    for z in range(1, sections):
        degree = degree + deg_all[z]
    inv = lax.rsqrt(1.0 + degree).T
    for b in range(blocks):
        scale[b * size:(b + 1) * size, :] = jnp.broadcast_to(inv[:, b:b + 1], (size, size))

    mine_at = pl.ds(pl.multiple_of(sec * span, span), span)
    total = part32[mine_at, :]
    for j in range(1, sections):
        peer = lax.rem(sec + j, sections)
        remote(rs_in.at[peer], rs_in.at[peer], rs_ssem.at[j], rs_rsem.at[peer], {"section": peer}).wait_recv()
        total = total + rs_in[peer].astype(jnp.float32)
    own_scale = scale[mine_at, :]
    aggregate = (total * jnp.concatenate([own_scale] * (width // size), axis=1)).astype(jnp.bfloat16)

    loads[1].wait()
    loads[2].wait()
    pre = jnp.dot(aggregate, w_v[...], preferred_element_type=jnp.float32)
    gate = jax.nn.sigmoid(pre)
    out[sec] = (pre * gate).astype(jnp.bfloat16)
    grad_pre = (cot_v[...].astype(jnp.float32) * gate * (1.0 + pre * (1.0 - gate))).astype(jnp.bfloat16)
    grad = lax.dot_general(aggregate, grad_pre, (((0,), (0,)), ((), ())), preferred_element_type=jnp.float32)
    grad = grad.reshape(rows, grain, width)
    gw32[...] = grad
    g_send[...] = grad.astype(jnp.bfloat16)

    tail = []
    for j in range(1, rows):
        peer = lax.rem(row + j, rows)
        d = remote(g_send.at[peer], ga_in.at[row], ga_ssem.at[j], ga_rsem.at[row], {"row": peer})
        d.start()
        tail.append(d)
    acc = gw32[row]
    for j in range(1, rows):
        peer = lax.rem(row + j, rows)
        remote(ga_in.at[peer], ga_in.at[peer], ga_ssem.at[j], ga_rsem.at[peer], {"row": peer}).wait_recv()
        acc = acc + ga_in[peer].astype(jnp.float32)
    gb_in[sec] = acc
    for j in range(1, sections):
        peer = lax.rem(sec + j, sections)
        d = remote(gb_in.at[sec], gb_in.at[sec], gb_ssem.at[j], gb_rsem.at[sec], {"section": peer})
        d.start()
        tail.append(d)
    out_copies = []
    for j in range(1, sections):
        peer = lax.rem(sec + j, sections)
        d = remote(out.at[sec], out.at[sec], o_ssem.at[j], o_rsem.at[sec], {"section": peer})
        d.start()
        out_copies.append(d)

    for j in range(1, sections):
        peer = lax.rem(sec + j, sections)
        remote(gb_in.at[peer], gb_in.at[peer], gb_ssem.at[j], gb_rsem.at[peer], {"section": peer}).wait_recv()
    acc = gb_in[0]
    for z in range(1, sections):
        acc = acc + gb_in[z]
    gw_out[row] = acc
    for j in range(1, rows):
        peer = lax.rem(row + j, rows)
        d = remote(gw_out.at[row], gw_out.at[row], gc_ssem.at[j], gc_rsem.at[row], {"row": peer})
        d.start()
        tail.append(d)
    for j in range(1, rows):
        peer = lax.rem(row + j, rows)
        remote(gw_out.at[peer], gw_out.at[peer], gc_ssem.at[j], gc_rsem.at[peer], {"row": peer}).wait_recv()
    for j in range(1, sections):
        peer = lax.rem(sec + j, sections)
        remote(out.at[peer], out.at[peer], o_ssem.at[j], o_rsem.at[peer], {"section": peer}).wait_recv()

    for cond, finish in sends:
        pl.when(cond)(finish)
    for d in deg_copies + rs_copies + out_copies + tail:
        d.wait_send()


def per_device(rows, sections, plane, features, weight, cotangent, counts, columns, live_slots):
    count, width = features.shape
    blocks, slots, size, _ = counts.shape
    span = count // sections
    grain = width // rows
    turns = rows // sections
    dma = pltpu.SemaphoreType.DMA
    f32, bf16 = jnp.float32, jnp.bfloat16
    any_spec = pl.BlockSpec(memory_space=pltpu.HBM)
    smem = pl.BlockSpec(memory_space=pltpu.SMEM)
    vmem = pl.BlockSpec(memory_space=pltpu.VMEM)
    out, grad = pl.pallas_call(
        functools.partial(kernel, rows, sections, plane),
        out_shape=(
            jax.ShapeDtypeStruct((sections, span, width), bf16),
            jax.ShapeDtypeStruct((rows, grain, width), f32),
        ),
        in_specs=[smem, smem, any_spec, any_spec, any_spec, any_spec],
        out_specs=(vmem, vmem),
        scratch_shapes=[
            pltpu.VMEM((blocks, slots, size, size), jnp.int32),
            pltpu.VMEM((span, width), bf16),
            pltpu.VMEM((width, width), bf16),
            pltpu.VMEM((blocks, size, slots * size), bf16),
            pltpu.VMEM((turns * blocks, size, width), bf16),
            pltpu.VMEM((sections, blocks, size), f32),
            pltpu.VMEM((count, size), f32),
            pltpu.VMEM((count, width), f32),
            pltpu.VMEM((count, width), bf16),
            pltpu.VMEM((sections, span, width), bf16),
            pltpu.VMEM((rows, grain, width), f32),
            pltpu.VMEM((rows, grain, width), bf16),
            pltpu.VMEM((rows, grain, width), bf16),
            pltpu.VMEM((sections, grain, width), f32),
            dma((4,)),
            dma((3, turns, blocks)) if plane else dma((turns, rows)),
            dma((turns, blocks)),
            dma((sections,)), dma((sections,)),
            dma((sections,)), dma((sections,)),
            dma((sections,)), dma((sections,)),
            dma((rows,)), dma((rows,)),
            dma((sections,)), dma((sections,)),
            dma((rows,)), dma((rows,)),
        ],
        compiler_params=pltpu.CompilerParams(
            collective_id=0, has_side_effects=True, vmem_limit_bytes=62 * 1024 * 1024
        ),
    )(
        live_slots.T, columns.T, features.reshape(blocks, size, width), weight,
        cotangent.reshape(sections, span, width), counts,
    )
    return out.reshape(count, width), grad.reshape(width, width)


def solution(mesh):
    rows, sections = mesh.shape["row"], mesh.shape["section"]
    in_specs = (
        P("row", None),
        P(),
        P("row", None),
        P("row", "section", None, None),
        P("row", "section"),
        P("row", "section"),
    )
    out_specs = (P("row", None), P())
    return jax.shard_map(
        functools.partial(per_device, rows, sections, (rows, sections) == (8, 4)),
        mesh=mesh, in_specs=in_specs, out_specs=out_specs, check_vma=False,
    )
```

```python
import functools

import jax
import jax.numpy as jnp
from jax import lax
from jax.experimental import pallas as pl
from jax.experimental.pallas import tpu as pltpu
from jax.sharding import PartitionSpec as P

MESH = pl.DeviceIdType.MESH


def remote(src, dst, send_sem, recv_sem, where):
    return pltpu.make_async_remote_copy(
        src_ref=src, dst_ref=dst, send_sem=send_sem, recv_sem=recv_sem,
        device_id=where, device_id_type=MESH,
    )


def kernel(
    rows, sections, plane,
    live, cols, feat, weight, cot, counts,
    out, gw_out,
    cnt_v, cot_v, w_v, edge, win, deg_all, scale, part32, part16, rs_in,
    gw32, ga_in, gb_in,
    l_sem, f_ssem, f_rsem, d_ssem, d_rsem, rs_ssem, rs_rsem, o_ssem, o_rsem,
    ga_ssem, ga_rsem, gb_ssem, gb_rsem, gc_ssem, gc_rsem,
):
    row = lax.axis_index("row")
    sec = lax.axis_index("section")
    blocks, slots, size, _ = cnt_v.shape
    width = win.shape[-1]
    turns = rows // sections
    span = rs_in.shape[1]
    grain = gw_out.shape[1]

    loads = [
        pltpu.make_async_copy(counts, cnt_v, l_sem.at[0]),
        pltpu.make_async_copy(weight, w_v, l_sem.at[1]),
        pltpu.make_async_copy(cot.at[sec], cot_v, l_sem.at[2]),
    ]
    for load in loads:
        load.start()

    barrier = pltpu.get_barrier_semaphore()
    for j in range(1, rows):
        pl.semaphore_signal(barrier, inc=1, device_id={"row": lax.rem(row + j, rows)}, device_id_type=MESH)
    for j in range(1, sections):
        pl.semaphore_signal(barrier, inc=1, device_id={"section": lax.rem(sec + j, sections)}, device_id_type=MESH)
    pl.semaphore_wait(barrier, rows - 1 + sections - 1)

    own = [row == t * sections + sec for t in range(turns)]
    keep = [pltpu.make_async_copy(feat, win.at[pl.ds(t * blocks, blocks)], l_sem.at[3]) for t in range(turns)]
    sends = []
    if plane:
        half = blocks // 2
        y, x, c = row // 4, lax.rem(row // 2, 2), lax.rem(row, 2)
        home_x = sec // 2
        sib = row + 1 - 2 * c

        def chunk(t, i, kind, where):
            return remote(
                win.at[t * blocks + i], win.at[t * blocks + i],
                f_ssem.at[kind, t, i], f_rsem.at[t, i], {"row": where},
            )

        for t in range(turns):
            def first(t=t, act="start"):
                for k in range(half):
                    for h in range(2):
                        i = h * half + k
                        for kind, where in (
                            (0, (1 - y) * 4 + x * 2 + h),
                            (1, y * 4 + (1 - x) * 2 + h),
                            (2, sib),
                        ):
                            d = remote(
                                feat.at[i], win.at[t * blocks + i],
                                f_ssem.at[kind, t, i], f_rsem.at[t, i], {"row": where},
                            )
                            if act == "start":
                                d.start()
                            else:
                                d.wait_send()

            @pl.when(own[t])
            def _(first=first, t=t):
                keep[t].start()
                first()

            sends.append((own[t], functools.partial(first, act="wait")))
    else:
        for t in range(turns):
            def direct(j, t):
                return remote(
                    feat, win.at[pl.ds(t * blocks, blocks)],
                    f_ssem.at[t, j], f_rsem.at[t, 0], {"row": lax.rem(row + j, rows)},
                )

            def first(act, t=t, direct=direct):
                def body(j, carry):
                    d = direct(j, t)
                    if act == "start":
                        d.start()
                    else:
                        d.wait_send()
                    return carry
                lax.fori_loop(1, rows, body, 0)

            @pl.when(own[t])
            def _(first=first, t=t):
                keep[t].start()
                first("start")

            sends.append((own[t], functools.partial(first, "wait")))

    loads[0].wait()
    ones = jnp.ones((8, size), jnp.bfloat16)

    def prepare(b, carry):
        total = jnp.zeros((size, size), jnp.int32)
        for k in range(slots):
            e = jnp.where(k < live[0, b], cnt_v[b, k], 0)
            total = total + e
            edge[b, :, k * size:(k + 1) * size] = e.astype(jnp.float32).astype(jnp.bfloat16)
        d = lax.dot_general(
            ones, total.astype(jnp.float32).astype(jnp.bfloat16), (((1,), (1,)), ((), ())),
            preferred_element_type=jnp.float32,
        )
        deg_all[sec, pl.ds(b, 1), :] = d[0:1]
        return carry

    lax.fori_loop(0, blocks, prepare, 0)
    deg_copies = []
    for j in range(1, sections):
        peer = lax.rem(sec + j, sections)
        d = remote(deg_all.at[sec], deg_all.at[sec], d_ssem.at[j], d_rsem.at[sec], {"section": peer})
        d.start()
        deg_copies.append(d)

    if plane:
        across = (1 - y) * 4 + x * 2 + c
        away = x != home_x
        far = 1 - y

        @pl.when(away)
        def _():
            for k in range(half):
                i = c * half + k
                chunk(y, i, 2, sib).wait_recv()
                chunk(y, i, 0, across).start()
                chunk(y, i, 2, sib).start()

        for k in range(half):
            i = c * half + k
            chunk(far, i, 2, sib).wait_recv()
            chunk(far, i, 2, sib).start()
        for k in range(half):
            chunk(far, (1 - c) * half + k, 2, sib).wait_recv()

        @pl.when(away)
        def _():
            for k in range(half):
                chunk(y, (1 - c) * half + k, 2, sib).wait_recv()

        @pl.when((x == home_x) & (c != lax.rem(sec, 2)))
        def _():
            for i in range(blocks):
                chunk(y, i, 2, sib).wait_recv()

        for t in range(turns):
            @pl.when(own[t])
            def _(t=t):
                keep[t].wait()

        def crossed():
            for k in range(half):
                chunk(y, c * half + k, 0, across).wait_send()
                chunk(y, c * half + k, 2, sib).wait_send()

        def relayed():
            for k in range(half):
                chunk(far, c * half + k, 2, sib).wait_send()

        sends.append((away, crossed))
        sends.append((row >= 0, relayed))
    else:
        for t in range(turns):
            @pl.when(own[t])
            def _(t=t):
                keep[t].wait()

            @pl.when(jnp.logical_not(own[t]))
            def _(t=t):
                direct(1, t).wait_recv()

    def block_sum(b):
        acc = jnp.zeros((size, width), jnp.float32)
        for k in range(0, slots, 2):
            picked = []
            for q in (k, k + 1):
                g = cols[q, b]
                picked.append(win[lax.div(lax.div(g, blocks), sections) * blocks + lax.rem(g, blocks)])
            acc = acc + jnp.dot(
                edge[b, :, k * size:(k + 2) * size], jnp.concatenate(picked, axis=0),
                preferred_element_type=jnp.float32,
            )
        at = pl.ds(pl.multiple_of(b * size, size), size)
        part32[at, :] = acc
        part16[at, :] = acc.astype(jnp.bfloat16)

    per = span // size
    if per == 0:
        for b in range(blocks):
            block_sum(b)
    rs_copies = []
    for j in range(1, sections + 1):
        peer = lax.rem(sec + j, sections)
        for q in range(per):
            block_sum(peer * per + q)
        if j < sections:
            d = remote(
                part16.at[pl.ds(pl.multiple_of(peer * span, span), span)], rs_in.at[sec],
                rs_ssem.at[j], rs_rsem.at[sec], {"section": peer},
            )
            d.start()
            rs_copies.append(d)

    for j in range(1, sections):
        peer = lax.rem(sec + j, sections)
        remote(deg_all.at[peer], deg_all.at[peer], d_ssem.at[j], d_rsem.at[peer], {"section": peer}).wait_recv()
    degree = deg_all[0]
    for z in range(1, sections):
        degree = degree + deg_all[z]
    inv = lax.rsqrt(1.0 + degree).T
    for b in range(blocks):
        scale[b * size:(b + 1) * size, :] = jnp.broadcast_to(inv[:, b:b + 1], (size, size))

    mine_at = pl.ds(pl.multiple_of(sec * span, span), span)
    total = part32[mine_at, :]
    for j in range(1, sections):
        peer = lax.rem(sec + j, sections)
        remote(rs_in.at[peer], rs_in.at[peer], rs_ssem.at[j], rs_rsem.at[peer], {"section": peer}).wait_recv()
        total = total + rs_in[peer].astype(jnp.float32)
    own_scale = scale[mine_at, :]
    aggregate = (total * jnp.concatenate([own_scale] * (width // size), axis=1)).astype(jnp.bfloat16)

    loads[1].wait()
    loads[2].wait()
    pre = jnp.dot(aggregate, w_v[...], preferred_element_type=jnp.float32)
    gate = jax.nn.sigmoid(pre)
    out[sec] = (pre * gate).astype(jnp.bfloat16)
    grad_pre = (cot_v[...].astype(jnp.float32) * gate * (1.0 + pre * (1.0 - gate))).astype(jnp.bfloat16)
    grad = lax.dot_general(aggregate, grad_pre, (((0,), (0,)), ((), ())), preferred_element_type=jnp.float32)
    grad = grad.reshape(rows, grain, width)
    gw32[...] = grad

    out_copies = []
    if plane:
        inner = (sec == 1) | (sec == 2)
        mate = sec + 1 - 2 * lax.rem(sec, 2)
        other_side = 2 - 2 * (sec // 2)
        targets = [2 - sec // 2, mate]
    else:
        targets = [lax.rem(sec + j, sections) for j in range(1, sections)]
    for j, peer in enumerate(targets):
        d = remote(out.at[sec], out.at[sec], o_ssem.at[j], o_rsem.at[sec], {"section": peer})
        d.start()
        out_copies.append(d)

    tail = []
    for j in range(1, rows):
        peer = lax.rem(row + j, rows)
        d = remote(gw32.at[peer], ga_in.at[row], ga_ssem.at[j], ga_rsem.at[row], {"row": peer})
        d.start()
        tail.append(d)
    acc = gw32[row]
    for j in range(1, rows):
        peer = lax.rem(row + j, rows)
        remote(ga_in.at[peer], ga_in.at[peer], ga_ssem.at[j], ga_rsem.at[peer], {"row": peer}).wait_recv()
        acc = acc + ga_in[peer]
    gb_in[sec] = acc.astype(jnp.bfloat16)
    for j in range(1, sections):
        peer = lax.rem(sec + j, sections)
        d = remote(gb_in.at[sec], gb_in.at[sec], gb_ssem.at[j], gb_rsem.at[sec], {"section": peer})
        d.start()
        tail.append(d)
    if plane:
        @pl.when(inner)
        def _():
            for q in range(2):
                at = other_side + q
                carry = remote(out.at[at], out.at[at], o_ssem.at[2 + q], o_rsem.at[at], {"section": mate})
                carry.wait_recv()
                carry.start()

    for j in range(1, sections):
        peer = lax.rem(sec + j, sections)
        remote(gb_in.at[peer], gb_in.at[peer], gb_ssem.at[j], gb_rsem.at[peer], {"section": peer}).wait_recv()
    acc = gb_in[0].astype(jnp.float32)
    for z in range(1, sections):
        acc = acc + gb_in[z].astype(jnp.float32)
    gw_out[row] = acc
    for j in range(1, rows):
        peer = lax.rem(row + j, rows)
        d = remote(gw_out.at[row], gw_out.at[row], gc_ssem.at[j], gc_rsem.at[row], {"row": peer})
        d.start()
        tail.append(d)
    for j in range(1, rows):
        peer = lax.rem(row + j, rows)
        remote(gw_out.at[peer], gw_out.at[peer], gc_ssem.at[j], gc_rsem.at[peer], {"row": peer}).wait_recv()
    def landed(at):
        remote(out.at[at], out.at[at], o_ssem.at[0], o_rsem.at[at], {"section": lax.rem(sec + 1, sections)}).wait_recv()

    if plane:
        landed(mate)

        @pl.when(jnp.logical_not(inner))
        def _():
            for q in range(2):
                landed(other_side + q)

        @pl.when(inner)
        def _():
            for q in range(2):
                at = other_side + q
                remote(out.at[at], out.at[at], o_ssem.at[2 + q], o_rsem.at[at], {"section": mate}).wait_send()
    else:
        for j in range(1, sections):
            landed(lax.rem(sec + j, sections))

    for cond, finish in sends:
        pl.when(cond)(finish)
    for d in deg_copies + rs_copies + out_copies + tail:
        d.wait_send()


def per_device(rows, sections, plane, features, weight, cotangent, counts, columns, live_slots):
    count, width = features.shape
    blocks, slots, size, _ = counts.shape
    span = count // sections
    grain = width // rows
    turns = rows // sections
    dma = pltpu.SemaphoreType.DMA
    f32, bf16 = jnp.float32, jnp.bfloat16
    any_spec = pl.BlockSpec(memory_space=pltpu.HBM)
    smem = pl.BlockSpec(memory_space=pltpu.SMEM)
    vmem = pl.BlockSpec(memory_space=pltpu.VMEM)
    out, grad = pl.pallas_call(
        functools.partial(kernel, rows, sections, plane),
        out_shape=(
            jax.ShapeDtypeStruct((sections, span, width), bf16),
            jax.ShapeDtypeStruct((rows, grain, width), f32),
        ),
        in_specs=[smem, smem, any_spec, any_spec, any_spec, any_spec],
        out_specs=(vmem, vmem),
        scratch_shapes=[
            pltpu.VMEM((blocks, slots, size, size), jnp.int32),
            pltpu.VMEM((span, width), bf16),
            pltpu.VMEM((width, width), bf16),
            pltpu.VMEM((blocks, size, slots * size), bf16),
            pltpu.VMEM((turns * blocks, size, width), bf16),
            pltpu.VMEM((sections, blocks, size), f32),
            pltpu.VMEM((count, size), f32),
            pltpu.VMEM((count, width), f32),
            pltpu.VMEM((count, width), bf16),
            pltpu.VMEM((sections, span, width), bf16),
            pltpu.VMEM((rows, grain, width), f32),
            pltpu.VMEM((rows, grain, width), f32),
            pltpu.VMEM((sections, grain, width), bf16),
            dma((4,)),
            dma((3, turns, blocks)) if plane else dma((turns, rows)),
            dma((turns, blocks)),
            dma((sections,)), dma((sections,)),
            dma((sections,)), dma((sections,)),
            dma((sections,)), dma((sections,)),
            dma((rows,)), dma((rows,)),
            dma((sections,)), dma((sections,)),
            dma((rows,)), dma((rows,)),
        ],
        compiler_params=pltpu.CompilerParams(
            collective_id=0, has_side_effects=True, vmem_limit_bytes=62 * 1024 * 1024
        ),
    )(
        live_slots.T, columns.T, features.reshape(blocks, size, width), weight,
        cotangent.reshape(sections, span, width), counts,
    )
    return out.reshape(count, width), grad.reshape(width, width)


def solution(mesh):
    rows, sections = mesh.shape["row"], mesh.shape["section"]
    in_specs = (
        P("row", None),
        P(),
        P("row", None),
        P("row", "section", None, None),
        P("row", "section"),
        P("row", "section"),
    )
    out_specs = (P("row", None), P())
    return jax.shard_map(
        functools.partial(per_device, rows, sections, (rows, sections) == (8, 4)),
        mesh=mesh, in_specs=in_specs, out_specs=out_specs, check_vma=False,
    )
```

```python
import functools

import jax
import jax.numpy as jnp
from jax import lax
from jax.experimental import pallas as pl
from jax.experimental.pallas import tpu as pltpu
from jax.sharding import PartitionSpec as P

MESH = pl.DeviceIdType.MESH


def remote(src, dst, send_sem, recv_sem, where):
    return pltpu.make_async_remote_copy(
        src_ref=src, dst_ref=dst, send_sem=send_sem, recv_sem=recv_sem,
        device_id=where, device_id_type=MESH,
    )


def kernel(
    rows, sections, plane,
    live, cols, feat, weight, cot, counts,
    out, gw_out,
    cnt_v, cot_v, w_v, edge, win, deg_all, scale, part32, part16, rs_in,
    gw32, ga_in, gb_in,
    l_sem, f_ssem, f_rsem, d_ssem, d_rsem, rs_ssem, rs_rsem, o_ssem, o_rsem,
    ga_ssem, ga_rsem, gb_ssem, gb_rsem, gc_ssem, gc_rsem,
):
    row = lax.axis_index("row")
    sec = lax.axis_index("section")
    blocks, slots, size, _ = cnt_v.shape
    width = win.shape[-1]
    turns = rows // sections
    span = rs_in.shape[1]
    grain = gw_out.shape[1]

    loads = [
        pltpu.make_async_copy(counts, cnt_v, l_sem.at[0]),
        pltpu.make_async_copy(weight, w_v, l_sem.at[1]),
        pltpu.make_async_copy(cot.at[sec], cot_v, l_sem.at[2]),
    ]
    for load in loads:
        load.start()

    barrier = pltpu.get_barrier_semaphore()
    for j in range(1, rows):
        pl.semaphore_signal(barrier, inc=1, device_id={"row": lax.rem(row + j, rows)}, device_id_type=MESH)
    for j in range(1, sections):
        pl.semaphore_signal(barrier, inc=1, device_id={"section": lax.rem(sec + j, sections)}, device_id_type=MESH)
    pl.semaphore_wait(barrier, rows - 1 + sections - 1)

    own = [row == t * sections + sec for t in range(turns)]
    keep = [pltpu.make_async_copy(feat, win.at[pl.ds(t * blocks, blocks)], l_sem.at[3]) for t in range(turns)]
    sends = []
    if plane:
        half = blocks // 2
        y, x, c = row // 4, lax.rem(row // 2, 2), lax.rem(row, 2)
        home_x = sec // 2
        sib = row + 1 - 2 * c

        def chunk(t, i, kind, where):
            return remote(
                win.at[t * blocks + i], win.at[t * blocks + i],
                f_ssem.at[kind, t, i], f_rsem.at[t, i], {"row": where},
            )

        for t in range(turns):
            def first(t=t, act="start"):
                for k in range(half):
                    for h in range(2):
                        i = h * half + k
                        for kind, where in (
                            (0, (1 - y) * 4 + x * 2 + h),
                            (1, y * 4 + (1 - x) * 2 + h),
                            (2, sib),
                        ):
                            d = remote(
                                feat.at[i], win.at[t * blocks + i],
                                f_ssem.at[kind, t, i], f_rsem.at[t, i], {"row": where},
                            )
                            if act == "start":
                                d.start()
                            else:
                                d.wait_send()

            @pl.when(own[t])
            def _(first=first, t=t):
                keep[t].start()
                first()

            sends.append((own[t], functools.partial(first, act="wait")))
    else:
        for t in range(turns):
            def direct(j, t):
                return remote(
                    feat, win.at[pl.ds(t * blocks, blocks)],
                    f_ssem.at[t, j], f_rsem.at[t, 0], {"row": lax.rem(row + j, rows)},
                )

            def first(act, t=t, direct=direct):
                def body(j, carry):
                    d = direct(j, t)
                    if act == "start":
                        d.start()
                    else:
                        d.wait_send()
                    return carry
                lax.fori_loop(1, rows, body, 0)

            @pl.when(own[t])
            def _(first=first, t=t):
                keep[t].start()
                first("start")

            sends.append((own[t], functools.partial(first, "wait")))

    loads[0].wait()
    ones = jnp.ones((8, size), jnp.bfloat16)

    def prepare(b, carry):
        total = jnp.zeros((size, size), jnp.int32)
        for k in range(slots):
            e = jnp.where(k < live[0, b], cnt_v[b, k], 0)
            total = total + e
            edge[b, :, k * size:(k + 1) * size] = e.astype(jnp.float32).astype(jnp.bfloat16)
        d = lax.dot_general(
            ones, total.astype(jnp.float32).astype(jnp.bfloat16), (((1,), (1,)), ((), ())),
            preferred_element_type=jnp.float32,
        )
        deg_all[sec, pl.ds(b, 1), :] = d[0:1]
        return carry

    lax.fori_loop(0, blocks, prepare, 0)
    deg_copies = []
    for j in range(1, sections):
        peer = lax.rem(sec + j, sections)
        d = remote(deg_all.at[sec], deg_all.at[sec], d_ssem.at[j], d_rsem.at[sec], {"section": peer})
        d.start()
        deg_copies.append(d)

    if plane:
        across = (1 - y) * 4 + x * 2 + c
        away = x != home_x
        far = 1 - y

        @pl.when(away)
        def _():
            for k in range(half):
                i = c * half + k
                chunk(y, i, 2, sib).wait_recv()
                chunk(y, i, 0, across).start()
                chunk(y, i, 2, sib).start()

        for k in range(half):
            i = c * half + k
            chunk(far, i, 2, sib).wait_recv()
            chunk(far, i, 2, sib).start()
        for k in range(half):
            chunk(far, (1 - c) * half + k, 2, sib).wait_recv()

        @pl.when(away)
        def _():
            for k in range(half):
                chunk(y, (1 - c) * half + k, 2, sib).wait_recv()

        @pl.when((x == home_x) & (c != lax.rem(sec, 2)))
        def _():
            for i in range(blocks):
                chunk(y, i, 2, sib).wait_recv()

        for t in range(turns):
            @pl.when(own[t])
            def _(t=t):
                keep[t].wait()

        def crossed():
            for k in range(half):
                chunk(y, c * half + k, 0, across).wait_send()
                chunk(y, c * half + k, 2, sib).wait_send()

        def relayed():
            for k in range(half):
                chunk(far, c * half + k, 2, sib).wait_send()

        sends.append((away, crossed))
        sends.append((row >= 0, relayed))
    else:
        for t in range(turns):
            @pl.when(own[t])
            def _(t=t):
                keep[t].wait()

            @pl.when(jnp.logical_not(own[t]))
            def _(t=t):
                direct(1, t).wait_recv()

    def block_sum(b):
        acc = jnp.zeros((size, width), jnp.float32)
        for k in range(0, slots, 2):
            picked = []
            for q in (k, k + 1):
                g = cols[q, b]
                picked.append(win[lax.div(lax.div(g, blocks), sections) * blocks + lax.rem(g, blocks)])
            acc = acc + jnp.dot(
                edge[b, :, k * size:(k + 2) * size], jnp.concatenate(picked, axis=0),
                preferred_element_type=jnp.float32,
            )
        at = pl.ds(pl.multiple_of(b * size, size), size)
        part32[at, :] = acc
        part16[at, :] = acc.astype(jnp.bfloat16)

    per = span // size
    if per == 0:
        for b in range(blocks):
            block_sum(b)
    rs_copies = []
    for j in range(1, sections + 1):
        peer = lax.rem(sec + j, sections)
        for q in range(per):
            block_sum(peer * per + q)
        if j < sections:
            d = remote(
                part16.at[pl.ds(pl.multiple_of(peer * span, span), span)], rs_in.at[sec],
                rs_ssem.at[j], rs_rsem.at[sec], {"section": peer},
            )
            d.start()
            rs_copies.append(d)

    for j in range(1, sections):
        peer = lax.rem(sec + j, sections)
        remote(deg_all.at[peer], deg_all.at[peer], d_ssem.at[j], d_rsem.at[peer], {"section": peer}).wait_recv()
    degree = deg_all[0]
    for z in range(1, sections):
        degree = degree + deg_all[z]
    inv = lax.rsqrt(1.0 + degree).T
    for b in range(blocks):
        scale[b * size:(b + 1) * size, :] = jnp.broadcast_to(inv[:, b:b + 1], (size, size))

    mine_at = pl.ds(pl.multiple_of(sec * span, span), span)
    total = part32[mine_at, :]
    for j in range(1, sections):
        peer = lax.rem(sec + j, sections)
        remote(rs_in.at[peer], rs_in.at[peer], rs_ssem.at[j], rs_rsem.at[peer], {"section": peer}).wait_recv()
        total = total + rs_in[peer].astype(jnp.float32)
    own_scale = scale[mine_at, :]
    aggregate = (total * jnp.concatenate([own_scale] * (width // size), axis=1)).astype(jnp.bfloat16)

    loads[1].wait()
    loads[2].wait()
    pre = jnp.dot(aggregate, w_v[...], preferred_element_type=jnp.float32)
    gate = jax.nn.sigmoid(pre)
    out[sec] = (pre * gate).astype(jnp.bfloat16)
    grad_pre = (cot_v[...].astype(jnp.float32) * gate * (1.0 + pre * (1.0 - gate))).astype(jnp.bfloat16)
    grad = lax.dot_general(aggregate, grad_pre, (((0,), (0,)), ((), ())), preferred_element_type=jnp.float32)
    grad = grad.reshape(rows, grain, width)
    gw32[...] = grad

    out_copies = []
    if plane:
        inner = (sec == 1) | (sec == 2)
        mate = sec + 1 - 2 * lax.rem(sec, 2)
        other_side = 2 - 2 * (sec // 2)
        targets = [2 - sec // 2, mate]
    else:
        targets = [lax.rem(sec + j, sections) for j in range(1, sections)]
    for j, peer in enumerate(targets):
        d = remote(out.at[sec], out.at[sec], o_ssem.at[j], o_rsem.at[sec], {"section": peer})
        d.start()
        out_copies.append(d)

    tail = []
    for j in range(1, rows):
        peer = lax.rem(row + j, rows)
        d = remote(gw32.at[peer], ga_in.at[row], ga_ssem.at[j], ga_rsem.at[row], {"row": peer})
        d.start()
        tail.append(d)
    acc = gw32[row]
    for j in range(1, rows):
        peer = lax.rem(row + j, rows)
        remote(ga_in.at[peer], ga_in.at[peer], ga_ssem.at[j], ga_rsem.at[peer], {"row": peer}).wait_recv()
        acc = acc + ga_in[peer]
    gb_in[sec] = acc.astype(jnp.bfloat16)
    for j in range(1, sections):
        peer = lax.rem(sec + j, sections)
        d = remote(gb_in.at[sec], gb_in.at[sec], gb_ssem.at[j], gb_rsem.at[sec], {"section": peer})
        d.start()
        tail.append(d)
    if plane:
        @pl.when(inner)
        def _():
            for q in range(2):
                at = other_side + q
                carry = remote(out.at[at], out.at[at], o_ssem.at[2 + q], o_rsem.at[at], {"section": mate})
                carry.wait_recv()
                carry.start()

    for j in range(1, sections):
        peer = lax.rem(sec + j, sections)
        remote(gb_in.at[peer], gb_in.at[peer], gb_ssem.at[j], gb_rsem.at[peer], {"section": peer}).wait_recv()
    acc = gb_in[0].astype(jnp.float32)
    for z in range(1, sections):
        acc = acc + gb_in[z].astype(jnp.float32)
    gw_out[row] = acc
    for j in range(1, rows):
        peer = lax.rem(row + j, rows)
        d = remote(gw_out.at[row], gw_out.at[row], gc_ssem.at[j], gc_rsem.at[row], {"row": peer})
        d.start()
        tail.append(d)
    for j in range(1, rows):
        peer = lax.rem(row + j, rows)
        remote(gw_out.at[peer], gw_out.at[peer], gc_ssem.at[j], gc_rsem.at[peer], {"row": peer}).wait_recv()
    def landed(at):
        remote(out.at[at], out.at[at], o_ssem.at[0], o_rsem.at[at], {"section": lax.rem(sec + 1, sections)}).wait_recv()

    if plane:
        landed(mate)

        @pl.when(jnp.logical_not(inner))
        def _():
            for q in range(2):
                landed(other_side + q)

        @pl.when(inner)
        def _():
            for q in range(2):
                at = other_side + q
                remote(out.at[at], out.at[at], o_ssem.at[2 + q], o_rsem.at[at], {"section": mate}).wait_send()
    else:
        for j in range(1, sections):
            landed(lax.rem(sec + j, sections))

    for cond, finish in sends:
        pl.when(cond)(finish)
    for d in deg_copies + rs_copies + out_copies + tail:
        d.wait_send()


def per_device(rows, sections, plane, features, weight, cotangent, counts, columns, live_slots):
    count, width = features.shape
    blocks, slots, size, _ = counts.shape
    span = count // sections
    grain = width // rows
    turns = rows // sections
    dma = pltpu.SemaphoreType.DMA
    f32, bf16 = jnp.float32, jnp.bfloat16
    pin = lambda a: pltpu.with_memory_space_constraint(a, pltpu.HBM)
    any_spec = pl.BlockSpec(memory_space=pltpu.HBM)
    smem = pl.BlockSpec(memory_space=pltpu.SMEM)
    vmem = pl.BlockSpec(memory_space=pltpu.VMEM)
    out, grad = pl.pallas_call(
        functools.partial(kernel, rows, sections, plane),
        out_shape=(
            jax.ShapeDtypeStruct((sections, span, width), bf16),
            jax.ShapeDtypeStruct((rows, grain, width), f32),
        ),
        in_specs=[smem, smem, any_spec, any_spec, any_spec, any_spec],
        out_specs=(vmem, vmem),
        scratch_shapes=[
            pltpu.VMEM((blocks, slots, size, size), jnp.int32),
            pltpu.VMEM((span, width), bf16),
            pltpu.VMEM((width, width), bf16),
            pltpu.VMEM((blocks, size, slots * size), bf16),
            pltpu.VMEM((turns * blocks, size, width), bf16),
            pltpu.VMEM((sections, blocks, size), f32),
            pltpu.VMEM((count, size), f32),
            pltpu.VMEM((count, width), f32),
            pltpu.VMEM((count, width), bf16),
            pltpu.VMEM((sections, span, width), bf16),
            pltpu.VMEM((rows, grain, width), f32),
            pltpu.VMEM((rows, grain, width), f32),
            pltpu.VMEM((sections, grain, width), bf16),
            dma((4,)),
            dma((3, turns, blocks)) if plane else dma((turns, rows)),
            dma((turns, blocks)),
            dma((sections,)), dma((sections,)),
            dma((sections,)), dma((sections,)),
            dma((sections,)), dma((sections,)),
            dma((rows,)), dma((rows,)),
            dma((sections,)), dma((sections,)),
            dma((rows,)), dma((rows,)),
        ],
        compiler_params=pltpu.CompilerParams(
            collective_id=0, has_side_effects=True, vmem_limit_bytes=40 * 1024 * 1024
        ),
    )(
        pin(live_slots.T), pin(columns.T), pin(features.reshape(blocks, size, width)), pin(weight),
        pin(cotangent.reshape(sections, span, width)), pin(counts),
    )
    return out.reshape(count, width), grad.reshape(width, width)


def solution(mesh):
    rows, sections = mesh.shape["row"], mesh.shape["section"]
    in_specs = (
        P("row", None),
        P(),
        P("row", None),
        P("row", "section", None, None),
        P("row", "section"),
        P("row", "section"),
    )
    out_specs = (P("row", None), P())
    return jax.shard_map(
        functools.partial(per_device, rows, sections, (rows, sections) == (8, 4)),
        mesh=mesh, in_specs=in_specs, out_specs=out_specs, check_vma=False,
    )
```

```python
import functools

import jax
import jax.numpy as jnp
from jax import lax
from jax.experimental import pallas as pl
from jax.experimental.pallas import tpu as pltpu
from jax.sharding import PartitionSpec as P

MESH = pl.DeviceIdType.MESH


def remote(src, dst, send_sem, recv_sem, where):
    return pltpu.make_async_remote_copy(
        src_ref=src, dst_ref=dst, send_sem=send_sem, recv_sem=recv_sem,
        device_id=where, device_id_type=MESH,
    )


def kernel(
    rows, sections, plane,
    live, cols, feat, weight, cot, counts,
    out, gw_out,
    cnt_v, cot_v, w_v, edge, win, deg_all, scale, part32, part16, rs_in,
    gw32, ga_in, gb_in,
    l_sem, f_ssem, f_rsem, d_ssem, d_rsem, rs_ssem, rs_rsem, o_ssem, o_rsem,
    ga_ssem, ga_rsem, gb_ssem, gb_rsem, gc_ssem, gc_rsem,
):
    row = lax.axis_index("row")
    sec = lax.axis_index("section")
    blocks, slots, size, _ = cnt_v.shape
    width = win.shape[-1]
    turns = rows // sections
    span = rs_in.shape[1]
    grain = gw_out.shape[1]

    loads = [
        pltpu.make_async_copy(counts, cnt_v, l_sem.at[0]),
        pltpu.make_async_copy(weight, w_v, l_sem.at[1]),
        pltpu.make_async_copy(cot.at[sec], cot_v, l_sem.at[2]),
    ]
    for load in loads:
        load.start()

    barrier = pltpu.get_barrier_semaphore()
    for j in range(1, rows):
        pl.semaphore_signal(barrier, inc=1, device_id={"row": lax.rem(row + j, rows)}, device_id_type=MESH)
    for j in range(1, sections):
        pl.semaphore_signal(barrier, inc=1, device_id={"section": lax.rem(sec + j, sections)}, device_id_type=MESH)
    pl.semaphore_wait(barrier, rows - 1 + sections - 1)

    own = [row == t * sections + sec for t in range(turns)]
    keep = [pltpu.make_async_copy(feat, win.at[pl.ds(t * blocks, blocks)], l_sem.at[3]) for t in range(turns)]
    sends = []
    if plane:
        half = blocks // 2
        y, x, c = row // 4, lax.rem(row // 2, 2), lax.rem(row, 2)
        home_x = sec // 2
        sib = row + 1 - 2 * c

        def chunk(t, i, kind, where):
            return remote(
                win.at[t * blocks + i], win.at[t * blocks + i],
                f_ssem.at[kind, t, i], f_rsem.at[t, i], {"row": where},
            )

        for t in range(turns):
            def first(t=t, act="start"):
                for k in range(half):
                    for h in range(2):
                        i = h * half + k
                        for kind, where in (
                            (0, (1 - y) * 4 + x * 2 + h),
                            (1, y * 4 + (1 - x) * 2 + h),
                            (2, sib),
                        ):
                            d = remote(
                                feat.at[i], win.at[t * blocks + i],
                                f_ssem.at[kind, t, i], f_rsem.at[t, i], {"row": where},
                            )
                            if act == "start":
                                d.start()
                            else:
                                d.wait_send()

            @pl.when(own[t])
            def _(first=first, t=t):
                keep[t].start()
                first()

            sends.append((own[t], functools.partial(first, act="wait")))
    else:
        for t in range(turns):
            def direct(j, t):
                return remote(
                    feat, win.at[pl.ds(t * blocks, blocks)],
                    f_ssem.at[t, j], f_rsem.at[t, 0], {"row": lax.rem(row + j, rows)},
                )

            def first(act, t=t, direct=direct):
                def body(j, carry):
                    d = direct(j, t)
                    if act == "start":
                        d.start()
                    else:
                        d.wait_send()
                    return carry
                lax.fori_loop(1, rows, body, 0)

            @pl.when(own[t])
            def _(first=first, t=t):
                keep[t].start()
                first("start")

            sends.append((own[t], functools.partial(first, "wait")))

    loads[0].wait()
    ones = jnp.ones((8, size), jnp.bfloat16)

    def prepare(b, carry):
        total = jnp.zeros((size, size), jnp.int32)
        for k in range(slots):
            e = jnp.where(k < live[0, b], cnt_v[b, k], 0)
            total = total + e
            edge[b, :, k * size:(k + 1) * size] = e.astype(jnp.float32).astype(jnp.bfloat16)
        d = lax.dot_general(
            ones, total.astype(jnp.float32).astype(jnp.bfloat16), (((1,), (1,)), ((), ())),
            preferred_element_type=jnp.float32,
        )
        deg_all[sec, pl.ds(b, 1), :] = d[0:1]
        return carry

    lax.fori_loop(0, blocks, prepare, 0)
    deg_copies = []
    for j in range(1, sections):
        peer = lax.rem(sec + j, sections)
        d = remote(deg_all.at[sec], deg_all.at[sec], d_ssem.at[j], d_rsem.at[sec], {"section": peer})
        d.start()
        deg_copies.append(d)

    if plane:
        across = (1 - y) * 4 + x * 2 + c
        away = x != home_x
        far = 1 - y

        @pl.when(away)
        def _():
            for k in range(half):
                i = c * half + k
                chunk(y, i, 2, sib).wait_recv()
                chunk(y, i, 0, across).start()
                chunk(y, i, 2, sib).start()

        for k in range(half):
            i = c * half + k
            chunk(far, i, 2, sib).wait_recv()
            chunk(far, i, 2, sib).start()
        for k in range(half):
            chunk(far, (1 - c) * half + k, 2, sib).wait_recv()

        @pl.when(away)
        def _():
            for k in range(half):
                chunk(y, (1 - c) * half + k, 2, sib).wait_recv()

        @pl.when((x == home_x) & (c != lax.rem(sec, 2)))
        def _():
            for i in range(blocks):
                chunk(y, i, 2, sib).wait_recv()

        for t in range(turns):
            @pl.when(own[t])
            def _(t=t):
                keep[t].wait()

        def crossed():
            for k in range(half):
                chunk(y, c * half + k, 0, across).wait_send()
                chunk(y, c * half + k, 2, sib).wait_send()

        def relayed():
            for k in range(half):
                chunk(far, c * half + k, 2, sib).wait_send()

        sends.append((away, crossed))
        sends.append((row >= 0, relayed))
    else:
        for t in range(turns):
            @pl.when(own[t])
            def _(t=t):
                keep[t].wait()

            @pl.when(jnp.logical_not(own[t]))
            def _(t=t):
                direct(1, t).wait_recv()

    def block_sum(b):
        acc = jnp.zeros((size, width), jnp.float32)
        for k in range(0, slots, 2):
            picked = []
            for q in (k, k + 1):
                g = cols[q, b]
                picked.append(win[lax.div(lax.div(g, blocks), sections) * blocks + lax.rem(g, blocks)])
            acc = acc + jnp.dot(
                edge[b, :, k * size:(k + 2) * size], jnp.concatenate(picked, axis=0),
                preferred_element_type=jnp.float32,
            )
        at = pl.ds(pl.multiple_of(b * size, size), size)
        part32[at, :] = acc
        part16[at, :] = acc.astype(jnp.bfloat16)

    per = span // size
    if per == 0:
        for b in range(blocks):
            block_sum(b)
    rs_copies = []
    order = [lax.rem(sec + j, sections) for j in range(1, sections + 1)]
    if plane:
        order = [sec + 2 - 4 * (sec // 2), 3 - sec, sec + 1 - 2 * lax.rem(sec, 2), sec]
    for j, peer in enumerate(order, 1):
        for q in range(per):
            block_sum(peer * per + q)
        if j < sections:
            d = remote(
                part16.at[pl.ds(pl.multiple_of(peer * span, span), span)], rs_in.at[sec],
                rs_ssem.at[j], rs_rsem.at[sec], {"section": peer},
            )
            d.start()
            rs_copies.append(d)

    for j in range(1, sections):
        peer = lax.rem(sec + j, sections)
        remote(deg_all.at[peer], deg_all.at[peer], d_ssem.at[j], d_rsem.at[peer], {"section": peer}).wait_recv()
    degree = deg_all[0]
    for z in range(1, sections):
        degree = degree + deg_all[z]
    inv = lax.rsqrt(1.0 + degree).T
    for b in range(blocks):
        scale[b * size:(b + 1) * size, :] = jnp.broadcast_to(inv[:, b:b + 1], (size, size))

    mine_at = pl.ds(pl.multiple_of(sec * span, span), span)
    total = part32[mine_at, :]
    for j in range(1, sections):
        peer = lax.rem(sec + j, sections)
        remote(rs_in.at[peer], rs_in.at[peer], rs_ssem.at[j], rs_rsem.at[peer], {"section": peer}).wait_recv()
        total = total + rs_in[peer].astype(jnp.float32)
    own_scale = scale[mine_at, :]
    aggregate = (total * jnp.concatenate([own_scale] * (width // size), axis=1)).astype(jnp.bfloat16)

    loads[1].wait()
    loads[2].wait()
    pre = jnp.dot(aggregate, w_v[...], preferred_element_type=jnp.float32)
    gate = jax.nn.sigmoid(pre)
    out[sec] = (pre * gate).astype(jnp.bfloat16)
    grad_pre = (cot_v[...].astype(jnp.float32) * gate * (1.0 + pre * (1.0 - gate))).astype(jnp.bfloat16)
    grad = lax.dot_general(aggregate, grad_pre, (((0,), (0,)), ((), ())), preferred_element_type=jnp.float32)
    grad = grad.reshape(rows, grain, width)
    gw32[...] = grad

    out_copies = []
    if plane:
        inner = (sec == 1) | (sec == 2)
        mate = sec + 1 - 2 * lax.rem(sec, 2)
        other_side = 2 - 2 * (sec // 2)
        targets = [2 - sec // 2, mate]
    else:
        targets = [lax.rem(sec + j, sections) for j in range(1, sections)]
    for j, peer in enumerate(targets):
        d = remote(out.at[sec], out.at[sec], o_ssem.at[j], o_rsem.at[sec], {"section": peer})
        d.start()
        out_copies.append(d)

    tail = []
    for j in range(1, rows):
        peer = lax.rem(row + j, rows)
        d = remote(gw32.at[peer], ga_in.at[row], ga_ssem.at[j], ga_rsem.at[row], {"row": peer})
        d.start()
        tail.append(d)
    acc = gw32[row]
    for j in range(1, rows):
        peer = lax.rem(row + j, rows)
        remote(ga_in.at[peer], ga_in.at[peer], ga_ssem.at[j], ga_rsem.at[peer], {"row": peer}).wait_recv()
        acc = acc + ga_in[peer]
    gb_in[sec] = acc.astype(jnp.bfloat16)
    for j in range(1, sections):
        peer = lax.rem(sec + j, sections)
        d = remote(gb_in.at[sec], gb_in.at[sec], gb_ssem.at[j], gb_rsem.at[sec], {"section": peer})
        d.start()
        tail.append(d)
    if plane:
        @pl.when(inner)
        def _():
            for q in range(2):
                at = other_side + q
                carry = remote(out.at[at], out.at[at], o_ssem.at[2 + q], o_rsem.at[at], {"section": mate})
                carry.wait_recv()
                carry.start()

    for j in range(1, sections):
        peer = lax.rem(sec + j, sections)
        remote(gb_in.at[peer], gb_in.at[peer], gb_ssem.at[j], gb_rsem.at[peer], {"section": peer}).wait_recv()
    acc = gb_in[0].astype(jnp.float32)
    for z in range(1, sections):
        acc = acc + gb_in[z].astype(jnp.float32)
    gw_out[row] = acc
    for j in range(1, rows):
        peer = lax.rem(row + j, rows)
        d = remote(gw_out.at[row], gw_out.at[row], gc_ssem.at[j], gc_rsem.at[row], {"row": peer})
        d.start()
        tail.append(d)
    for j in range(1, rows):
        peer = lax.rem(row + j, rows)
        remote(gw_out.at[peer], gw_out.at[peer], gc_ssem.at[j], gc_rsem.at[peer], {"row": peer}).wait_recv()
    def landed(at):
        remote(out.at[at], out.at[at], o_ssem.at[0], o_rsem.at[at], {"section": lax.rem(sec + 1, sections)}).wait_recv()

    if plane:
        landed(mate)

        @pl.when(jnp.logical_not(inner))
        def _():
            for q in range(2):
                landed(other_side + q)

        @pl.when(inner)
        def _():
            for q in range(2):
                at = other_side + q
                remote(out.at[at], out.at[at], o_ssem.at[2 + q], o_rsem.at[at], {"section": mate}).wait_send()
    else:
        for j in range(1, sections):
            landed(lax.rem(sec + j, sections))

    for cond, finish in sends:
        pl.when(cond)(finish)
    for d in deg_copies + rs_copies + out_copies + tail:
        d.wait_send()


def per_device(rows, sections, plane, features, weight, cotangent, counts, columns, live_slots):
    count, width = features.shape
    blocks, slots, size, _ = counts.shape
    span = count // sections
    grain = width // rows
    turns = rows // sections
    dma = pltpu.SemaphoreType.DMA
    f32, bf16 = jnp.float32, jnp.bfloat16
    pin = lambda a: pltpu.with_memory_space_constraint(a, pltpu.HBM)
    any_spec = pl.BlockSpec(memory_space=pltpu.HBM)
    smem = pl.BlockSpec(memory_space=pltpu.SMEM)
    vmem = pl.BlockSpec(memory_space=pltpu.VMEM)
    out, grad = pl.pallas_call(
        functools.partial(kernel, rows, sections, plane),
        out_shape=(
            jax.ShapeDtypeStruct((sections, span, width), bf16),
            jax.ShapeDtypeStruct((rows, grain, width), f32),
        ),
        in_specs=[smem, smem, any_spec, any_spec, any_spec, any_spec],
        out_specs=(vmem, vmem),
        scratch_shapes=[
            pltpu.VMEM((blocks, slots, size, size), jnp.int32),
            pltpu.VMEM((span, width), bf16),
            pltpu.VMEM((width, width), bf16),
            pltpu.VMEM((blocks, size, slots * size), bf16),
            pltpu.VMEM((turns * blocks, size, width), bf16),
            pltpu.VMEM((sections, blocks, size), f32),
            pltpu.VMEM((count, size), f32),
            pltpu.VMEM((count, width), f32),
            pltpu.VMEM((count, width), bf16),
            pltpu.VMEM((sections, span, width), bf16),
            pltpu.VMEM((rows, grain, width), f32),
            pltpu.VMEM((rows, grain, width), f32),
            pltpu.VMEM((sections, grain, width), bf16),
            dma((4,)),
            dma((3, turns, blocks)) if plane else dma((turns, rows)),
            dma((turns, blocks)),
            dma((sections,)), dma((sections,)),
            dma((sections,)), dma((sections,)),
            dma((sections,)), dma((sections,)),
            dma((rows,)), dma((rows,)),
            dma((sections,)), dma((sections,)),
            dma((rows,)), dma((rows,)),
        ],
        compiler_params=pltpu.CompilerParams(
            collective_id=0, has_side_effects=True, vmem_limit_bytes=40 * 1024 * 1024
        ),
    )(
        pin(live_slots.T), pin(columns.T), pin(features.reshape(blocks, size, width)), pin(weight),
        pin(cotangent.reshape(sections, span, width)), pin(counts),
    )
    return out.reshape(count, width), grad.reshape(width, width)


def solution(mesh):
    rows, sections = mesh.shape["row"], mesh.shape["section"]
    in_specs = (
        P("row", None),
        P(),
        P("row", None),
        P("row", "section", None, None),
        P("row", "section"),
        P("row", "section"),
    )
    out_specs = (P("row", None), P())
    return jax.shard_map(
        functools.partial(per_device, rows, sections, (rows, sections) == (8, 4)),
        mesh=mesh, in_specs=in_specs, out_specs=out_specs, check_vma=False,
    )
```
